32 devices in a mesh: op: 16 (over z, x, core), sec: 2 (over y).
Axes of the slice: x: 2, y: 2, z: 4, core: 2. Of those that a mesh axis runs over, the one named last changes fastest.
Arguments:
- left_ops: float32 [16, 2, 1024, 1024], P('op', 'sec'), may hold values from -0.5 to 3.5
- right_ops: float32 [16, 2, 1024, 1024], P('op', 'sec'), may hold values from -0.5 to 3.5
- amplitudes: float32 [2, 1024, 1024], P('sec', 'op'), may hold values from -72 to 72
- sketch: float32 [1024, 512], replicated, may hold values from -0.1875 to 0.1875
- sector_shift: int32 [16], P('op'), may hold values from 0 to 3
Outputs:
- rotated: float32 [16, 2, 512, 512], P('op', 'sec')
- new_basis: float32 [2, 1024, 512], P('sec', 'op')
- energy: float32 [], replicated
The draws below stay inside these ranges and needn't reach their ends.
Inputs may be any that keep to these rules, and one draw needn't show every extreme that they name: The target sector of pair k from source sector s is (s + sector_shift[k]) mod 2.
All inputs are finite; a program needn't handle non-finite values.
Results may differ from the reference program's by a relative error of at most 0.0003.
Values sent between devices are 32-bit elements; how exact they have to be, the bound alone decides.
A program may use at most 128 MiB of HBM per device.

```python
import jax
import jax.numpy as jnp
from jax import lax

M = 1024
KEEP = 512
PAIRS = 16
SECTORS = 2


def dominant(key):
    key_diag, key_rest = jax.random.split(key)
    jitter = jnp.clip(jax.random.normal(key_rest, (PAIRS, SECTORS, M, M), jnp.float32), -6.0, 6.0)
    diagonal = 10.0 ** jax.random.uniform(key_diag, (PAIRS, SECTORS, M, 1), jnp.float32, -0.3, 0.3)
    identity = jnp.eye(M, dtype=jnp.float32)
    return jitter * (0.5 * M ** (-0.5)) + identity * diagonal


def draw_left_ops(key, part):
    return dominant(jax.random.fold_in(key, 101))


def draw_right_ops(key, part):
    return dominant(jax.random.fold_in(key, 202))


def draw_amplitudes(key, part):
    key_jitter, key_rows, key_cols = jax.random.split(jax.random.fold_in(key, 303), 3)
    jitter = jnp.clip(jax.random.normal(key_jitter, (SECTORS, M, M), jnp.float32), -6.0, 6.0)
    rising = 10.0 ** (jnp.arange(M, dtype=jnp.float32) / M)
    row_rough = jax.random.uniform(key_rows, (SECTORS, M, 1), jnp.float32, 0.5, 1.5)
    col_scale = 10.0 ** jax.random.uniform(key_cols, (SECTORS, 1, M), jnp.float32, 0.0, 0.5)
    return jitter * rising[None, :, None] * row_rough * col_scale / 4.0


def with_ends(result, key, low, largest):
    longest = result.shape.index(max(result.shape))
    spots = []
    for shift in (0, 1):
        where = [jax.random.randint(jax.random.fold_in(key, axis), (), 0, length) for axis, length in enumerate(result.shape)]
        where[longest] = (where[longest] + shift) % result.shape[longest]
        spots.append(tuple(where))
    return result.at[spots[0]].set(low).at[spots[1]].set(largest)


def centred(own_key, extent, scale, limit, kind=jnp.bfloat16):
    entries = jax.random.normal(own_key, extent, jnp.float32) * scale
    return jnp.minimum(jnp.maximum(entries, -limit), limit).astype(kind)


def setup_inputs(seed: int = 0) -> dict:
    arg_keys = jax.random.split(jax.random.key(seed), 6)
    return {
        "left_ops": draw_left_ops(jax.random.fold_in(arg_keys[5], 71), 0),
        "right_ops": draw_right_ops(jax.random.fold_in(arg_keys[5], 71), 0),
        "amplitudes": draw_amplitudes(jax.random.fold_in(arg_keys[5], 71), 0),
        "sketch": centred(arg_keys[3], (M, KEEP), M ** -0.5, 0.1875, jnp.float32),
        "sector_shift": with_ends(jax.random.randint(arg_keys[4], (PAIRS,), 0, 4), jax.random.fold_in(arg_keys[4], 1), 0, 3).astype(jnp.int32),
    }


EXACT = lax.Precision.HIGHEST

def solve_one(factor_one, sketch_one):
    return jax.scipy.linalg.solve_triangular(factor_one, sketch_one.T, lower=True).T

def reference(left_ops, right_ops, amplitudes, sketch, sector_shift):

    def add_pair(running, inputs):
        left_pair, right_pair, offset = inputs

        def per_sector(sector):
            right_part = jnp.dot(amplitudes[sector].astype(jnp.float32), right_pair[sector].astype(jnp.float32), precision=EXACT, preferred_element_type=jnp.float32)
            return jnp.dot(left_pair[sector].astype(jnp.float32), right_part.astype(jnp.float32), precision=EXACT, preferred_element_type=jnp.float32)
        sector_terms = lax.map(per_sector, jnp.arange(SECTORS, dtype=jnp.int32))
        return (running + jnp.roll(sector_terms, offset, axis=0), None)
    product, unused_out = lax.scan(add_pair, jnp.zeros_like(amplitudes), (left_ops, right_ops, sector_shift))
    correlation = jnp.sum(amplitudes * product)
    norm_sq = jnp.sum(amplitudes * amplitudes)
    energy = correlation / norm_sq
    residual = product - energy * amplitudes
    sketched = jnp.einsum('smn,nk->smk', residual, sketch, precision=EXACT)
    gram_mat = jnp.einsum('smk,sml->skl', sketched, sketched, precision=EXACT)
    factor = jnp.linalg.cholesky(gram_mat)
    new_basis = jax.vmap(solve_one)(factor, sketched)

    def rotate(carried, inputs):
        left_pair, offset = inputs
        applied = jnp.einsum('smn,snk->smk', left_pair, new_basis, precision=EXACT)
        target = jnp.roll(new_basis, -offset, axis=0)
        return (carried, jnp.einsum('smk,sml->skl', target, applied, precision=EXACT))
    carried_out, rotated = lax.scan(rotate, jnp.zeros((), jnp.float32), (left_ops, sector_shift))
    return (rotated, new_basis, energy)
```

```python
import functools

import jax
import jax.numpy as jnp
from jax import lax
from jax.experimental import pallas as pl
from jax.experimental.pallas import tpu as pltpu
from jax.sharding import PartitionSpec as P

EXACT = lax.Precision.HIGHEST
SPLIT = lax.Precision.HIGH
HALF = 64
BLOCK = 128


def matmul(first, second, precision=SPLIT):
    return jnp.dot(first, second, precision=precision, preferred_element_type=jnp.float32)


def exact_nn(first, second):
    return lax.dot_general(first, second, (((1,), (0,)), ((), ())), precision=EXACT, preferred_element_type=jnp.float32)


def exact_nt(first, second):
    return lax.dot_general(first, second, (((1,), (1,)), ((), ())), precision=EXACT, preferred_element_type=jnp.float32)


def eliminate_many(blocks):
    sub = lax.broadcasted_iota(jnp.int32, (8, BLOCK), 0)
    lane = lax.broadcasted_iota(jnp.int32, (8, BLOCK), 1)
    rows = [[block[8 * c : 8 * c + 8, :] for c in range(HALF // 8)] for block in blocks]
    for j in range(HALF):
        home = j // 8
        for chunk in rows:
            row = chunk[home][j % 8 : j % 8 + 1, :]
            scaled = row / row[:, j : j + 1]
            for c in range(home, HALF // 8):
                column = jnp.broadcast_to(chunk[c][:, j : j + 1], (8, BLOCK))
                if c == home:
                    column = jnp.where(sub > j % 8, column, 0.0)
                chunk[c] = chunk[c] - column * scaled
    results = []
    for chunk in rows:
        scaled_chunks = []
        for c in range(HALF // 8):
            pivot = jnp.sum(jnp.where(lane == sub + 8 * c, chunk[c], 0.0), axis=1, keepdims=True)
            scaled_chunks.append(jnp.where(lane >= HALF, chunk[c] * lax.rsqrt(pivot), 0.0))
        results.append(jnp.concatenate(scaled_chunks, axis=0))
    return results


def invert_blocks(blocks):
    lane = lax.broadcasted_iota(jnp.int32, (HALF, BLOCK), 1)
    row = lax.broadcasted_iota(jnp.int32, (HALF, BLOCK), 0)
    unit = jnp.where(lane == row + HALF, 1.0, 0.0)
    empty = jnp.zeros((HALF, BLOCK), jnp.float32)

    def tall(top):
        return jnp.concatenate([top, empty], axis=0)

    first = eliminate_many([jnp.where(lane < HALF, block[:HALF], unit) for block in blocks])
    upper = [pltpu.roll(one, HALF, 1) for one in first]
    lower = [block[HALF:] for block in blocks]
    coupling = [exact_nt(low, tall(up)) for low, up in zip(lower, upper)]
    schur = [pltpu.roll(low, HALF, 1) - exact_nt(mid, tall(mid)) for low, mid in zip(lower, coupling)]
    second = eliminate_many([jnp.where(lane < HALF, one, unit) for one in schur])
    result = []
    for up, mid, right in zip(upper, coupling, second):
        carried = exact_nn(mid, tall(up))
        left = exact_nn(pltpu.roll(right, HALF, 1), tall(carried))
        result.append(jnp.concatenate([up, right - left], axis=0))
    return result


def inverse_factor_kernel(count, order, gram_ref, inverse_ref, work):
    row = lax.broadcasted_iota(jnp.int32, (order, order), 0)
    column = lax.broadcasted_iota(jnp.int32, (order, order), 1)
    for i in range(count):
        work[i] = gram_ref[i]
        inverse_ref[i] = jnp.where(row == column, 1.0, 0.0)
    tall_row = lax.broadcasted_iota(jnp.int32, (order, BLOCK), 0)

    def step(b, carry):
        start = pl.multiple_of(b * BLOCK, BLOCK)
        here = pl.ds(start, BLOCK)
        inverses = invert_blocks([work[i, here, here] for i in range(count)])
        for i in range(count):
            panel = jnp.where(tall_row >= start + BLOCK, work[i, :, here], 0.0)
            low = exact_nt(panel, inverses[i])
            strip = exact_nn(inverses[i], inverse_ref[i, here, :])
            inverse_ref[i] = inverse_ref[i] - exact_nn(low, strip)
            inverse_ref[i, here, :] = strip
            work[i] = work[i] - exact_nt(low, low)
        return carry

    lax.fori_loop(0, order // BLOCK, step, 0)


def inverse_factors(gram_pair):
    count, order, _ = gram_pair.shape
    return pl.pallas_call(
        functools.partial(inverse_factor_kernel, count, order),
        out_shape=jax.ShapeDtypeStruct(gram_pair.shape, jnp.float32),
        in_specs=[pl.BlockSpec(memory_space=pltpu.VMEM)],
        out_specs=pl.BlockSpec(memory_space=pltpu.VMEM),
        scratch_shapes=[pltpu.VMEM(gram_pair.shape, jnp.float32)],
        name="inverse_factors",
    )(gram_pair)


def body(left_ops, right_ops, amplitudes, sketch, sector_shift):
    left_op = left_ops[0, 0]
    right_op = right_ops[0, 0]
    state_slab = amplitudes[0]
    sectors = lax.axis_size("sec")
    slabs = lax.axis_size("op")
    height, width = state_slab.shape
    order = height * slabs
    keep = sketch.shape[1]
    source = lax.axis_index("sec")
    target = lax.rem(source + sector_shift[0], sectors)

    states = lax.all_gather(state_slab, ("sec", "op"), axis=0, tiled=True).reshape(sectors, order, width)
    right_sk = matmul(right_op, sketch)
    state_here = lax.dynamic_index_in_dim(states, source, 0, keepdims=False)
    term_sk = matmul(left_op, matmul(state_here, right_sk))
    mine = lax.broadcasted_iota(jnp.int32, (sectors, 1, 1), 0) == target
    spread = jnp.where(mine, term_sk[None], 0.0).reshape(sectors * order, keep)
    first_slab = lax.psum_scatter(spread, ("sec", "op"), scatter_dimension=0, tiled=True)

    state_there = lax.dynamic_index_in_dim(states, target, 0, keepdims=False)
    term_full = matmul(left_op, matmul(state_here, right_op))
    correlation = jnp.sum(state_there * term_full)
    norm_sq = jnp.sum(states * states)
    second_here = matmul(state_here, sketch)
    second_there = matmul(state_there, sketch)

    packed = jnp.concatenate([first_slab, jnp.full((8, keep), correlation, jnp.float32)], axis=0)
    gathered = lax.all_gather(packed, ("sec", "op"), axis=0, tiled=True).reshape(sectors, slabs, height + 8, keep)
    energy = jnp.sum(gathered[:, :, height, 0]) / norm_sq
    first_here = lax.dynamic_index_in_dim(gathered, source, 0, keepdims=False)[:, :height].reshape(order, keep)
    first_there = lax.dynamic_index_in_dim(gathered, target, 0, keepdims=False)[:, :height].reshape(order, keep)
    sketched = jnp.stack([first_here - energy * second_here, first_there - energy * second_there])
    gram_pair = jnp.einsum("srk,srl->skl", sketched, sketched, precision=EXACT)
    inverse_pair = inverse_factors(gram_pair)
    basis_here = lax.dot_general(sketched[0], inverse_pair[0], (((1,), (1,)), ((), ())), precision=SPLIT)
    basis_there = lax.dot_general(sketched[1], inverse_pair[1], (((1,), (1,)), ((), ())), precision=SPLIT)
    basis_slab = lax.dynamic_slice_in_dim(basis_here, lax.axis_index("op") * height, height, 0)
    applied = matmul(left_op, basis_here)
    rotated = jnp.einsum("rk,rl->kl", basis_there, applied, precision=SPLIT)
    return (rotated[None, None], basis_slab[None], energy)


def solution(mesh):
    in_specs = (
        P("op", "sec", None, None),
        P("op", "sec", None, None),
        P("sec", "op", None),
        P(),
        P("op"),
    )
    out_specs = (P("op", "sec", None, None), P("sec", "op", None), P())
    return jax.shard_map(body, mesh=mesh, in_specs=in_specs, out_specs=out_specs, check_vma=False)
```

```python
import functools

import jax
import jax.numpy as jnp
from jax import lax
from jax.experimental import pallas as pl
from jax.experimental.pallas import tpu as pltpu
from jax.sharding import PartitionSpec as P

EXACT = lax.Precision.HIGHEST
SPLIT = lax.Precision.HIGH
HALF = 64
BLOCK = 128


def matmul(first, second, precision=SPLIT):
    return jnp.dot(first, second, precision=precision, preferred_element_type=jnp.float32)


def exact_nn(first, second):
    return lax.dot_general(first, second, (((1,), (0,)), ((), ())), precision=EXACT, preferred_element_type=jnp.float32)


def exact_nt(first, second):
    return lax.dot_general(first, second, (((1,), (1,)), ((), ())), precision=EXACT, preferred_element_type=jnp.float32)


def eliminate_many(blocks):
    sub = lax.broadcasted_iota(jnp.int32, (8, BLOCK), 0)
    lane = lax.broadcasted_iota(jnp.int32, (8, BLOCK), 1)
    rows = [[block[8 * c : 8 * c + 8, :] for c in range(HALF // 8)] for block in blocks]
    for j in range(0, HALF, 2):
        home = j // 8
        for chunk in rows:
            row = chunk[home][j % 8 : j % 8 + 1, :]
            follower = chunk[home][j % 8 + 1 : j % 8 + 2, :]
            head = jnp.broadcast_to(row[:, j : j + 1], (1, BLOCK))
            cross = jnp.broadcast_to(row[:, j + 1 : j + 2], (1, BLOCK))
            tail = jnp.broadcast_to(follower[:, j + 1 : j + 2], (1, BLOCK))
            head_inverse = 1.0 / head
            ratio = cross * head_inverse
            scaled = row * head_inverse
            reduced = follower - cross * scaled
            reduced_scaled = reduced * (head / (head * tail - cross * cross))
            for c in range(home, HALF // 8):
                column = jnp.broadcast_to(chunk[c][:, j : j + 1], (8, BLOCK))
                beside = jnp.broadcast_to(chunk[c][:, j + 1 : j + 2], (8, BLOCK)) - column * ratio
                if c == home:
                    column = jnp.where(sub > j % 8, column, 0.0)
                    beside = jnp.where(sub > j % 8 + 1, beside, 0.0)
                chunk[c] = chunk[c] - column * scaled - beside * reduced_scaled
    results = []
    for chunk in rows:
        scaled_chunks = []
        for c in range(HALF // 8):
            pivot = jnp.sum(jnp.where(lane == sub + 8 * c, chunk[c], 0.0), axis=1, keepdims=True)
            scaled_chunks.append(jnp.where(lane >= HALF, chunk[c] * lax.rsqrt(pivot), 0.0))
        results.append(jnp.concatenate(scaled_chunks, axis=0))
    return results


def invert_blocks(blocks):
    lane = lax.broadcasted_iota(jnp.int32, (HALF, BLOCK), 1)
    row = lax.broadcasted_iota(jnp.int32, (HALF, BLOCK), 0)
    unit = jnp.where(lane == row + HALF, 1.0, 0.0)
    empty = jnp.zeros((HALF, BLOCK), jnp.float32)

    def tall(top):
        return jnp.concatenate([top, empty], axis=0)

    first = eliminate_many([jnp.where(lane < HALF, block[:HALF], unit) for block in blocks])
    upper = [pltpu.roll(one, HALF, 1) for one in first]
    lower = [block[HALF:] for block in blocks]
    coupling = [exact_nt(low, tall(up)) for low, up in zip(lower, upper)]
    schur = [pltpu.roll(low, HALF, 1) - exact_nt(mid, tall(mid)) for low, mid in zip(lower, coupling)]
    second = eliminate_many([jnp.where(lane < HALF, one, unit) for one in schur])
    result = []
    for up, mid, right in zip(upper, coupling, second):
        carried = exact_nn(mid, tall(up))
        left = exact_nn(pltpu.roll(right, HALF, 1), tall(carried))
        result.append(jnp.concatenate([up, right - left], axis=0))
    return result


def inverse_factor_kernel(count, order, gram_ref, inverse_ref, work):
    row = lax.broadcasted_iota(jnp.int32, (order, order), 0)
    column = lax.broadcasted_iota(jnp.int32, (order, order), 1)
    for i in range(count):
        work[i] = gram_ref[i]
        inverse_ref[i] = jnp.where(row == column, 1.0, 0.0)
    tall_row = lax.broadcasted_iota(jnp.int32, (order, BLOCK), 0)

    def step(b, carry):
        start = pl.multiple_of(b * BLOCK, BLOCK)
        here = pl.ds(start, BLOCK)
        inverses = invert_blocks([work[i, here, here] for i in range(count)])
        for i in range(count):
            panel = jnp.where(tall_row >= start + BLOCK, work[i, :, here], 0.0)
            low = exact_nt(panel, inverses[i])
            strip = exact_nn(inverses[i], inverse_ref[i, here, :])
            inverse_ref[i] = inverse_ref[i] - exact_nn(low, strip)
            inverse_ref[i, here, :] = strip
            work[i] = work[i] - exact_nt(low, low)
        return carry

    lax.fori_loop(0, order // BLOCK, step, 0)


def inverse_factors(gram_pair):
    count, order, _ = gram_pair.shape
    return pl.pallas_call(
        functools.partial(inverse_factor_kernel, count, order),
        out_shape=jax.ShapeDtypeStruct(gram_pair.shape, jnp.float32),
        in_specs=[pl.BlockSpec(memory_space=pltpu.VMEM)],
        out_specs=pl.BlockSpec(memory_space=pltpu.VMEM),
        scratch_shapes=[pltpu.VMEM(gram_pair.shape, jnp.float32)],
        cost_estimate=pl.CostEstimate(flops=40 * order**3, bytes_accessed=8 * order**2, transcendentals=0),
        name="inverse_factors",
    )(gram_pair)


def shifted(block, axis, distance):
    devices = range(lax.axis_size(axis))
    route = [((i - distance) % len(devices), i) for i in devices]
    return lax.ppermute(block, axis, route)


def from_target(block, choice, reach):
    result = block
    for distance in range(1, reach):
        result = jnp.where(choice == distance, shifted(block, "sec", -distance), result)
    return result


def from_target_halves(block, choice, reach):
    slabs = lax.axis_size("op")
    half = block.shape[0] // 2
    side = lax.rem(lax.axis_index("op"), 2)
    share = lax.dynamic_slice_in_dim(block, side * half, half, 0)
    result = block
    for distance in range(1, reach):
        mine = shifted(share, "sec", -distance)
        other = lax.ppermute(mine, "op", [(i, i ^ 1) for i in range(slabs)])
        whole = jnp.concatenate([jnp.where(side == 0, mine, other), jnp.where(side == 0, other, mine)], axis=0)
        result = jnp.where(choice == distance, whole, result)
    return result


def body(left_ops, right_ops, amplitudes, sketch, sector_shift):
    left_op = left_ops[0, 0]
    right_op = right_ops[0, 0]
    state_slab = amplitudes[0]
    sectors = lax.axis_size("sec")
    slabs = lax.axis_size("op")
    height = state_slab.shape[0]
    order = height * slabs
    keep = sketch.shape[1]
    choice = lax.rem(sector_shift[0], sectors)
    reach = min(4, sectors)

    state = lax.all_gather(state_slab, "op", axis=0, tiled=True)
    right_sk = matmul(right_op, sketch)
    term_sk = matmul(left_op, matmul(state, right_sk))
    spread = jnp.concatenate([jnp.where(choice == d, term_sk, 0.0) for d in range(reach)], axis=1)
    parts = lax.psum_scatter(spread, "op", scatter_dimension=0, tiled=True)

    state_there = from_target_halves(state, choice, reach)
    term_full = matmul(left_op, matmul(state, right_op))
    second_sk = matmul(state, sketch)
    lane = lax.broadcasted_iota(jnp.int32, (8, keep), 1)
    sums = jnp.where(lane == 0, jnp.sum(state_there * term_full), jnp.sum(state_slab * state_slab))
    all_sums = sums
    for distance in range(1, sectors):
        all_sums = all_sums + shifted(sums, "sec", distance)

    first_slab = parts[:, :keep]
    for distance in range(1, reach):
        first_slab = first_slab + shifted(parts[:, distance * keep : (distance + 1) * keep], "sec", distance)

    packed = jnp.concatenate([first_slab, all_sums], axis=0)
    gathered = lax.all_gather(packed, "op", axis=0, tiled=True).reshape(slabs, height + 8, keep)
    totals = jnp.sum(gathered[:, height, :2], axis=0)
    energy = totals[0] / totals[1]
    sketched = gathered[:, :height].reshape(order, keep) - energy * second_sk
    sketched_there = from_target(sketched, choice, reach)
    gram_mat = jnp.einsum("rk,rl->kl", sketched, sketched, precision=EXACT)
    inverse = inverse_factors(gram_mat[None])[0]
    inverse_there = from_target(inverse, choice, reach)
    basis = lax.dot_general(sketched, inverse, (((1,), (1,)), ((), ())), precision=SPLIT)
    basis_slab = lax.dynamic_slice_in_dim(basis, lax.axis_index("op") * height, height, 0)
    applied = matmul(left_op, basis)
    unscaled = jnp.einsum("rk,rl->kl", sketched_there, applied, precision=SPLIT)
    rotated = matmul(inverse_there, unscaled)
    return (rotated[None, None], basis_slab[None], energy)


def solution(mesh):
    in_specs = (
        P("op", "sec", None, None),
        P("op", "sec", None, None),
        P("sec", "op", None),
        P(),
        P("op"),
    )
    out_specs = (P("op", "sec", None, None), P("sec", "op", None), P())
    return jax.shard_map(body, mesh=mesh, in_specs=in_specs, out_specs=out_specs, check_vma=False)
```

```python
import functools

import jax
import jax.numpy as jnp
from jax import lax
from jax.experimental import pallas as pl
from jax.experimental.layout import Layout, with_layout_constraint
from jax.experimental.pallas import tpu as pltpu
from jax.sharding import PartitionSpec as P

EXACT = lax.Precision.HIGHEST
SPLIT = lax.Precision.HIGH
HALF = 64
BLOCK = 128


def matmul(first, second, precision=SPLIT):
    return jnp.dot(first, second, precision=precision, preferred_element_type=jnp.float32)


def exact_nn(first, second):
    return lax.dot_general(first, second, (((1,), (0,)), ((), ())), precision=EXACT, preferred_element_type=jnp.float32)


def exact_nt(first, second):
    return lax.dot_general(first, second, (((1,), (1,)), ((), ())), precision=EXACT, preferred_element_type=jnp.float32)


def eliminate_many(blocks):
    sub = lax.broadcasted_iota(jnp.int32, (8, BLOCK), 0)
    lane = lax.broadcasted_iota(jnp.int32, (8, BLOCK), 1)
    rows = [[block[8 * c : 8 * c + 8, :] for c in range(HALF // 8)] for block in blocks]
    for j in range(0, HALF, 2):
        home = j // 8
        for chunk in rows:
            row = chunk[home][j % 8 : j % 8 + 1, :]
            follower = chunk[home][j % 8 + 1 : j % 8 + 2, :]
            head = jnp.broadcast_to(row[:, j : j + 1], (1, BLOCK))
            cross = jnp.broadcast_to(row[:, j + 1 : j + 2], (1, BLOCK))
            tail = jnp.broadcast_to(follower[:, j + 1 : j + 2], (1, BLOCK))
            head_inverse = 1.0 / head
            ratio = cross * head_inverse
            scaled = row * head_inverse
            reduced = follower - cross * scaled
            reduced_scaled = reduced * (head / (head * tail - cross * cross))
            for c in range(home, HALF // 8):
                column = jnp.broadcast_to(chunk[c][:, j : j + 1], (8, BLOCK))
                beside = jnp.broadcast_to(chunk[c][:, j + 1 : j + 2], (8, BLOCK)) - column * ratio
                if c == home:
                    column = jnp.where(sub > j % 8, column, 0.0)
                    beside = jnp.where(sub > j % 8 + 1, beside, 0.0)
                chunk[c] = chunk[c] - column * scaled - beside * reduced_scaled
    results = []
    for chunk in rows:
        scaled_chunks = []
        for c in range(HALF // 8):
            pivot = jnp.sum(jnp.where(lane == sub + 8 * c, chunk[c], 0.0), axis=1, keepdims=True)
            scaled_chunks.append(jnp.where(lane >= HALF, chunk[c] * lax.rsqrt(pivot), 0.0))
        results.append(jnp.concatenate(scaled_chunks, axis=0))
    return results


def invert_blocks(blocks):
    lane = lax.broadcasted_iota(jnp.int32, (HALF, BLOCK), 1)
    row = lax.broadcasted_iota(jnp.int32, (HALF, BLOCK), 0)
    unit = jnp.where(lane == row + HALF, 1.0, 0.0)
    empty = jnp.zeros((HALF, BLOCK), jnp.float32)

    def tall(top):
        return jnp.concatenate([top, empty], axis=0)

    first = eliminate_many([jnp.where(lane < HALF, block[:HALF], unit) for block in blocks])
    upper = [pltpu.roll(one, HALF, 1) for one in first]
    lower = [block[HALF:] for block in blocks]
    coupling = [exact_nt(low, tall(up)) for low, up in zip(lower, upper)]
    schur = [pltpu.roll(low, HALF, 1) - exact_nt(mid, tall(mid)) for low, mid in zip(lower, coupling)]
    second = eliminate_many([jnp.where(lane < HALF, one, unit) for one in schur])
    result = []
    for up, mid, right in zip(upper, coupling, second):
        carried = exact_nn(mid, tall(up))
        left = exact_nn(pltpu.roll(right, HALF, 1), tall(carried))
        result.append(jnp.concatenate([up, right - left], axis=0))
    return result


def inverse_factor_kernel(count, order, gram_ref, inverse_ref, work):
    row = lax.broadcasted_iota(jnp.int32, (order, order), 0)
    column = lax.broadcasted_iota(jnp.int32, (order, order), 1)
    for i in range(count):
        work[i] = gram_ref[i]
        inverse_ref[i] = jnp.where(row == column, 1.0, 0.0)
    tall_row = lax.broadcasted_iota(jnp.int32, (order, BLOCK), 0)

    def step(b, carry):
        start = pl.multiple_of(b * BLOCK, BLOCK)
        here = pl.ds(start, BLOCK)
        inverses = invert_blocks([work[i, here, here] for i in range(count)])
        for i in range(count):
            panel = jnp.where(tall_row >= start + BLOCK, work[i, :, here], 0.0)
            low = exact_nt(panel, inverses[i])
            strip = exact_nn(inverses[i], inverse_ref[i, here, :])
            inverse_ref[i] = inverse_ref[i] - exact_nn(low, strip)
            inverse_ref[i, here, :] = strip
            work[i] = work[i] - exact_nt(low, low)
        return carry

    lax.fori_loop(0, order // BLOCK, step, 0)


def inverse_factors(gram_pair):
    count, order, _ = gram_pair.shape
    return pl.pallas_call(
        functools.partial(inverse_factor_kernel, count, order),
        out_shape=jax.ShapeDtypeStruct(gram_pair.shape, jnp.float32),
        in_specs=[pl.BlockSpec(memory_space=pltpu.VMEM)],
        out_specs=pl.BlockSpec(memory_space=pltpu.VMEM),
        scratch_shapes=[pltpu.VMEM(gram_pair.shape, jnp.float32)],
        cost_estimate=pl.CostEstimate(flops=40 * order**3, bytes_accessed=8 * order**2, transcendentals=0),
        name="inverse_factors",
    )(gram_pair)


def shifted(block, axis, distance):
    devices = range(lax.axis_size(axis))
    route = [((i - distance) % len(devices), i) for i in devices]
    return lax.ppermute(block, axis, route)


def from_target(block, choice, reach):
    result = block
    for distance in range(1, reach):
        result = jnp.where(choice == distance, shifted(block, "sec", -distance), result)
    return result


def row_major(block):
    return with_layout_constraint(block, Layout(major_to_minor=tuple(range(block.ndim))))


def from_target_halves(block, choice, reach, beside=()):
    slabs = lax.axis_size("op")
    half = block.shape[0] // 2
    side = lax.rem(lax.axis_index("op"), 2)
    share = row_major(lax.dynamic_slice_in_dim(block, side * half, half, 0))
    result = block
    for distance in range(1, reach):
        mine = shifted(share, "sec", -distance)
        if beside:
            mine, *beside = lax.optimization_barrier((mine, *beside))
        other = lax.ppermute(mine, "op", [(i, i ^ 1) for i in range(slabs)])
        whole = jnp.concatenate([jnp.where(side == 0, mine, other), jnp.where(side == 0, other, mine)], axis=0)
        result = jnp.where(choice == distance, whole, result)
    return result, beside


def body(left_ops, right_ops, amplitudes, sketch, sector_shift):
    left_op = left_ops[0, 0]
    right_op = right_ops[0, 0]
    state_slab = amplitudes[0]
    sectors = lax.axis_size("sec")
    slabs = lax.axis_size("op")
    height = state_slab.shape[0]
    order = height * slabs
    keep = sketch.shape[1]
    choice = lax.rem(sector_shift[0], sectors)
    reach = min(4, sectors)

    slab = lax.optimization_barrier(row_major(state_slab))
    state = row_major(lax.all_gather(slab, "op", axis=0, tiled=True))
    right_sk = matmul(right_op, sketch)
    term_sk = row_major(matmul(left_op, row_major(matmul(state, right_sk))))
    mark = lax.broadcasted_iota(jnp.int32, (1, reach, 1, 1), 1) == choice
    spread = jnp.where(mark, term_sk.reshape(slabs, 1, height, keep), 0.0).reshape(slabs * reach * height, keep)
    parts = lax.psum_scatter(spread, "op", scatter_dimension=0, tiled=True)

    term_full = matmul(left_op, row_major(matmul(state, right_op)))
    second_sk = matmul(state, sketch)
    state_there, (term_full, second_sk) = from_target_halves(state, choice, reach, (term_full, second_sk))
    lane = lax.broadcasted_iota(jnp.int32, (8, keep), 1)
    sums = jnp.where(lane == 0, jnp.sum(state_there * term_full), jnp.sum(state_slab * state_slab))
    all_sums = sums
    for distance in range(1, sectors):
        all_sums = all_sums + shifted(sums, "sec", distance)

    first_slab = parts[:height]
    for distance in range(1, reach):
        first_slab = first_slab + shifted(parts[distance * height : (distance + 1) * height], "sec", distance)

    packed = jnp.concatenate([first_slab, all_sums], axis=0)
    gathered = lax.all_gather(packed, "op", axis=0, tiled=True).reshape(slabs, height + 8, keep)
    totals = jnp.sum(gathered[:, height, :2], axis=0)
    energy = totals[0] / totals[1]
    sketched = gathered[:, :height].reshape(order, keep) - energy * second_sk
    sketched_there = from_target(sketched, choice, reach)
    gram_mat = jnp.einsum("rk,rl->kl", sketched, sketched, precision=EXACT)
    inverse = inverse_factors(gram_mat[None])[0]
    inverse_there, _ = from_target_halves(inverse, choice, reach)
    basis = lax.dot_general(sketched, inverse, (((1,), (1,)), ((), ())), precision=SPLIT)
    basis_slab = lax.dynamic_slice_in_dim(basis, lax.axis_index("op") * height, height, 0)
    applied = matmul(left_op, basis)
    unscaled = jnp.einsum("rk,rl->kl", sketched_there, applied, precision=SPLIT)
    rotated = matmul(inverse_there, unscaled)
    return (rotated[None, None], basis_slab[None], energy)


def solution(mesh):
    in_specs = (
        P("op", "sec", None, None),
        P("op", "sec", None, None),
        P("sec", "op", None),
        P(),
        P("op"),
    )
    out_specs = (P("op", "sec", None, None), P("sec", "op", None), P())
    return jax.shard_map(body, mesh=mesh, in_specs=in_specs, out_specs=out_specs, check_vma=False)
```

```python
import functools

import jax
import jax.numpy as jnp
from jax import lax
from jax.experimental import pallas as pl
from jax.experimental.layout import Layout, with_layout_constraint
from jax.experimental.pallas import tpu as pltpu
from jax.sharding import PartitionSpec as P

EXACT = lax.Precision.HIGHEST
SPLIT = lax.Precision.HIGH
HALF = 64
BLOCK = 128


def matmul(first, second, precision=SPLIT):
    return jnp.dot(first, second, precision=precision, preferred_element_type=jnp.float32)


def exact_nn(first, second):
    return lax.dot_general(first, second, (((1,), (0,)), ((), ())), precision=EXACT, preferred_element_type=jnp.float32)


def exact_nt(first, second):
    return lax.dot_general(first, second, (((1,), (1,)), ((), ())), precision=EXACT, preferred_element_type=jnp.float32)


def eliminate_many(blocks):
    sub = lax.broadcasted_iota(jnp.int32, (8, BLOCK), 0)
    lane = lax.broadcasted_iota(jnp.int32, (8, BLOCK), 1)
    rows = [[block[8 * c : 8 * c + 8, :] for c in range(HALF // 8)] for block in blocks]
    for j in range(0, HALF, 2):
        home = j // 8
        for chunk in rows:
            row = chunk[home][j % 8 : j % 8 + 1, :]
            follower = chunk[home][j % 8 + 1 : j % 8 + 2, :]
            head = jnp.broadcast_to(row[:, j : j + 1], (1, BLOCK))
            cross = jnp.broadcast_to(row[:, j + 1 : j + 2], (1, BLOCK))
            tail = jnp.broadcast_to(follower[:, j + 1 : j + 2], (1, BLOCK))
            head_inverse = 1.0 / head
            ratio = cross * head_inverse
            scaled = row * head_inverse
            reduced = follower - cross * scaled
            reduced_scaled = reduced * (head / (head * tail - cross * cross))
            for c in range(home, HALF // 8):
                column = jnp.broadcast_to(chunk[c][:, j : j + 1], (8, BLOCK))
                beside = jnp.broadcast_to(chunk[c][:, j + 1 : j + 2], (8, BLOCK)) - column * ratio
                if c == home:
                    column = jnp.where(sub > j % 8, column, 0.0)
                    beside = jnp.where(sub > j % 8 + 1, beside, 0.0)
                chunk[c] = chunk[c] - column * scaled - beside * reduced_scaled
    results = []
    for chunk in rows:
        scaled_chunks = []
        for c in range(HALF // 8):
            pivot = jnp.sum(jnp.where(lane == sub + 8 * c, chunk[c], 0.0), axis=1, keepdims=True)
            scaled_chunks.append(jnp.where(lane >= HALF, chunk[c] * lax.rsqrt(pivot), 0.0))
        results.append(jnp.concatenate(scaled_chunks, axis=0))
    return results


def invert_blocks(blocks):
    lane = lax.broadcasted_iota(jnp.int32, (HALF, BLOCK), 1)
    row = lax.broadcasted_iota(jnp.int32, (HALF, BLOCK), 0)
    unit = jnp.where(lane == row + HALF, 1.0, 0.0)
    empty = jnp.zeros((HALF, BLOCK), jnp.float32)

    def tall(top):
        return jnp.concatenate([top, empty], axis=0)

    first = eliminate_many([jnp.where(lane < HALF, block[:HALF], unit) for block in blocks])
    upper = [pltpu.roll(one, HALF, 1) for one in first]
    lower = [block[HALF:] for block in blocks]
    coupling = [exact_nt(low, tall(up)) for low, up in zip(lower, upper)]
    schur = [pltpu.roll(low, HALF, 1) - exact_nt(mid, tall(mid)) for low, mid in zip(lower, coupling)]
    second = eliminate_many([jnp.where(lane < HALF, one, unit) for one in schur])
    result = []
    for up, mid, right in zip(upper, coupling, second):
        carried = exact_nn(mid, tall(up))
        left = exact_nn(pltpu.roll(right, HALF, 1), tall(carried))
        result.append(jnp.concatenate([up, right - left], axis=0))
    return result


def inverse_factor_kernel(count, order, gram_ref, inverse_ref, work):
    row = lax.broadcasted_iota(jnp.int32, (order, order), 0)
    column = lax.broadcasted_iota(jnp.int32, (order, order), 1)
    for i in range(count):
        work[i] = gram_ref[i]
        inverse_ref[i] = jnp.where(row == column, 1.0, 0.0)
    tall_row = lax.broadcasted_iota(jnp.int32, (order, BLOCK), 0)

    def step(b, carry):
        start = pl.multiple_of(b * BLOCK, BLOCK)
        here = pl.ds(start, BLOCK)
        inverses = invert_blocks([work[i, here, here] for i in range(count)])
        for i in range(count):
            panel = jnp.where(tall_row >= start + BLOCK, work[i, :, here], 0.0)
            low = exact_nt(panel, inverses[i])
            strip = exact_nn(inverses[i], inverse_ref[i, here, :])
            inverse_ref[i] = inverse_ref[i] - exact_nn(low, strip)
            inverse_ref[i, here, :] = strip
            work[i] = work[i] - exact_nt(low, low)
        return carry

    lax.fori_loop(0, order // BLOCK, step, 0)


def inverse_factors(gram_pair):
    count, order, _ = gram_pair.shape
    return pl.pallas_call(
        functools.partial(inverse_factor_kernel, count, order),
        out_shape=jax.ShapeDtypeStruct(gram_pair.shape, jnp.float32),
        in_specs=[pl.BlockSpec(memory_space=pltpu.VMEM)],
        out_specs=pl.BlockSpec(memory_space=pltpu.VMEM),
        scratch_shapes=[pltpu.VMEM(gram_pair.shape, jnp.float32)],
        cost_estimate=pl.CostEstimate(flops=40 * order**3, bytes_accessed=8 * order**2, transcendentals=0),
        name="inverse_factors",
    )(gram_pair)


def shifted(block, axis, distance):
    devices = range(lax.axis_size(axis))
    route = [((i - distance) % len(devices), i) for i in devices]
    return lax.ppermute(block, axis, route)


def from_target(block, choice, reach):
    result = block
    for distance in range(1, reach):
        result = jnp.where(choice == distance, shifted(block, "sec", -distance), result)
    return result


def row_major(block):
    return with_layout_constraint(block, Layout(major_to_minor=tuple(range(block.ndim))))


def from_target_halves(block, choice, reach, beside=()):
    slabs = lax.axis_size("op")
    half = block.shape[0] // 2
    side = lax.rem(lax.axis_index("op"), 2)
    share = row_major(lax.dynamic_slice_in_dim(block, side * half, half, 0))
    result = block
    for distance in range(1, reach):
        mine = shifted(share, "sec", -distance)
        if beside:
            mine, *beside = lax.optimization_barrier((mine, *beside))
        other = lax.ppermute(mine, "op", [(i, i ^ 1) for i in range(slabs)])
        whole = jnp.concatenate([jnp.where(side == 0, mine, other), jnp.where(side == 0, other, mine)], axis=0)
        result = jnp.where(choice == distance, whole, result)
    return result, beside


def body(left_ops, right_ops, amplitudes, sketch, sector_shift):
    left_op = left_ops[0, 0]
    right_op = right_ops[0, 0]
    state_slab = amplitudes[0]
    sectors = lax.axis_size("sec")
    slabs = lax.axis_size("op")
    height = state_slab.shape[0]
    order = height * slabs
    keep = sketch.shape[1]
    choice = lax.rem(sector_shift[0], sectors)
    reach = min(4, sectors)

    slab = lax.optimization_barrier(row_major(state_slab))
    state = row_major(lax.all_gather(slab, "op", axis=0, tiled=True))
    right_sk = matmul(right_op, sketch)
    term_sk = row_major(matmul(left_op, row_major(matmul(state, right_sk))))
    mark = lax.broadcasted_iota(jnp.int32, (1, reach, 1, 1), 1) == choice
    spread = jnp.where(mark, term_sk.reshape(slabs, 1, height, keep), 0.0).reshape(slabs * reach * height, keep)
    parts = lax.psum_scatter(spread, "op", scatter_dimension=0, tiled=True)

    term_full = matmul(left_op, row_major(matmul(state, right_op)))
    second_sk = matmul(state, sketch)
    state_there, (term_full, second_sk) = from_target_halves(state, choice, reach, (term_full, second_sk))
    lane = lax.broadcasted_iota(jnp.int32, (8, keep), 1)
    sums = jnp.where(lane == 0, jnp.sum(state_there * term_full), jnp.sum(state_slab * state_slab))
    all_sums = sums
    for distance in range(1, sectors):
        all_sums = all_sums + shifted(sums, "sec", distance)

    first_slab = parts[:height]
    for distance in range(1, reach):
        first_slab = first_slab + shifted(parts[distance * height : (distance + 1) * height], "sec", distance)

    packed = jnp.concatenate([first_slab, all_sums], axis=0)
    gathered = lax.all_gather(packed, "op", axis=0, tiled=True).reshape(slabs, height + 8, keep)
    totals = jnp.sum(gathered[:, height, :2], axis=0)
    energy = totals[0] / totals[1]
    sketched = gathered[:, :height].reshape(order, keep) - energy * second_sk
    sketched_there = from_target(sketched, choice, reach)
    gram_mat = jnp.einsum("rk,rl->kl", sketched, sketched, precision=EXACT)
    inverse = inverse_factors(gram_mat[None])[0]
    basis = lax.dot_general(sketched, inverse, (((1,), (1,)), ((), ())), precision=SPLIT)
    basis_slab = lax.dynamic_slice_in_dim(basis, lax.axis_index("op") * height, height, 0)
    applied = matmul(left_op, basis)
    inverse_there, (applied,) = from_target_halves(inverse, choice, reach, (applied,))
    unscaled = jnp.einsum("rk,rl->kl", sketched_there, applied, precision=SPLIT)
    rotated = matmul(inverse_there, unscaled)
    return (rotated[None, None], basis_slab[None], energy)


def solution(mesh):
    in_specs = (
        P("op", "sec", None, None),
        P("op", "sec", None, None),
        P("sec", "op", None),
        P(),
        P("op"),
    )
    out_specs = (P("op", "sec", None, None), P("sec", "op", None), P())
    return jax.shard_map(body, mesh=mesh, in_specs=in_specs, out_specs=out_specs, check_vma=False)
```
